256 devices in a mesh: shard: 64 (over z, y_hi, x), tensor: 4 (over y_lo, core).
Axes of the slice: x: 4, y: 4 (y_hi: 2, y_lo: 2; y = y_hi * 2 + y_lo), z: 8, core: 2. Of those that a mesh axis runs over, the one named last changes fastest.
Arguments:
- acts: bfloat16 [131072, 2048], P('shard', 'tensor'), may hold values from -6 to 6
- out_grad: bfloat16 [131072, 1920], P('shard'), may hold values from -6 to 6
- sample_rows: int32 [4096], P('shard'), may hold values from 0 to 2047
- own_a: int32 [4, 4], replicated, may hold values from 0 to 3, each once within a row
- own_g: int32 [4, 5], replicated, may hold values from 0 to 4, each once within a row
- a_state: float32 [4, 4, 128, 128], P('tensor'), as said below
- g_state: float32 [4, 5, 96, 96], P('tensor'), as said below
- momentum: float32 [1920, 2048], P('shard', 'tensor'), may hold values from -6 to 6
- weight: float32 [1920, 2048], P('shard', 'tensor'), may hold values from -6 to 6
Outputs:
- a_state_new: float32 [4, 4, 128, 128], P('tensor')
- g_state_new: float32 [4, 5, 96, 96], P('tensor')
- momentum_new: float32 [1920, 2048], P('shard', 'tensor')
- weight_new: float32 [1920, 2048], P('shard', 'tensor')
- weight_bf16: bfloat16 [1920, 2048], P(None, 'tensor')
The draws below stay inside these ranges and needn't reach their ends.
Inputs may be any that keep to these rules, and one draw needn't show every extreme that they name: `own_a`: slot s of a group is owned by the shard index s times the whole part of the shard axis's size over the group's number of slots. `own_g`: slot s of a group is owned by the shard index s times the whole part of the shard axis's size over the group's number of slots. `a_state`: every slot is symmetric positive definite. `g_state`: every slot is symmetric positive definite.
All inputs are finite; a program needn't handle non-finite values. Where the reference program divides by a largest or mean magnitude, that divisor is 1e-20 or more.
Results may differ from the reference program's by a relative error of at most 0.0004.
Values may be sent and summed in bfloat16 or wider, within the bound.
A program may use at most 64 MiB of HBM per device.

```python
import math
import jax
import jax.numpy as jnp
from jax import lax

D = 2048
Q = 1920
BA = 128
BG = 96
TOK_DEV = 2048
S_DEV = 64
NS_IT = 5
TOKENS = 131072
SAMPLES = 4096
ABLK_T = 4
GBLK_T = 5
N_TENSOR = 4


def draw_factor(key, count, width):
    noise_key, diag_key = jax.random.split(key)
    noise = jax.random.normal(noise_key, (N_TENSOR, count, width, width), jnp.float32)
    spread = (noise + jnp.swapaxes(noise, -1, -2)) * (0.3 / math.sqrt(width))
    diagonal = jax.random.uniform(diag_key, (N_TENSOR, count, width), jnp.float32, 1.0, 3.0)
    return spread + diagonal[..., None] * jnp.eye(width, dtype=jnp.float32)


def draw_a_state(key, part):
    return draw_factor(jax.random.fold_in(key, 31), ABLK_T, BA)


def draw_g_state(key, part):
    return draw_factor(jax.random.fold_in(key, 47), GBLK_T, BG)


def plant(array, rng, smallest, top_value):
    spot = [jax.random.randint(jax.random.fold_in(rng, axis), (), 0, length) for axis, length in enumerate(array.shape)]
    longest = array.shape.index(max(array.shape))
    neighbour = spot[:longest] + [(spot[longest] + 1) % array.shape[longest]] + spot[longest + 1:]
    return array.at[tuple(spot)].set(smallest).at[tuple(neighbour)].set(top_value)


def shard_levels(stream_key, shape, shards, least, top_value):
    def one(dim, shards_of):
        draws = jax.random.uniform(jax.random.fold_in(jax.random.fold_in(stream_key, 6), dim), (shards_of,), jnp.float32, least / len(shards), top_value / len(shards))
        return jnp.repeat(jnp.exp(draws), shape[dim] // shards_of).reshape((-1,) + (1,) * (len(shape) - dim - 1))

    gain = one(*shards[0])
    for cut in shards[1:]:
        gain = gain * one(*cut)
    return gain


def normal_values(rng, shape, deviation, most, shards=(), kind=jnp.bfloat16):
    factor_of = shard_levels(rng, shape, shards, -0.22, 0.18) if shards else 1.0
    array = jax.random.normal(rng, shape, jnp.float32) * deviation * factor_of
    return jnp.minimum(jnp.maximum(array, -most), most).astype(kind)


def setup_inputs(seed: int = 0) -> dict:
    key_list = jax.random.split(jax.random.key(seed), 10)
    acts = normal_values(key_list[0], (TOKENS, D), 1.0, 6.0, ((0, 64), (1, 4)))
    out_grad = normal_values(key_list[1], (TOKENS, Q), 1.0, 6.0, ((0, 64),))
    sample_rows = plant(jax.random.randint(key_list[2], (SAMPLES,), 0, TOK_DEV), jax.random.fold_in(key_list[2], 1), 0, TOK_DEV - 1).astype(jnp.int32)
    own_a = jax.vmap(lambda own: jax.random.permutation(own, ABLK_T))(jax.random.split(key_list[3], N_TENSOR)).reshape((N_TENSOR, ABLK_T)).astype(jnp.int32)
    own_g = jax.vmap(lambda own: jax.random.permutation(own, GBLK_T))(jax.random.split(key_list[4], N_TENSOR)).reshape((N_TENSOR, GBLK_T)).astype(jnp.int32)
    a_state = draw_a_state(jax.random.fold_in(key_list[9], 71), 0)
    g_state = draw_g_state(jax.random.fold_in(key_list[9], 71), 0)
    momentum = normal_values(key_list[7], (Q, D), 1.0, 6.0, ((0, 64), (1, 4)), jnp.float32)
    weight = normal_values(key_list[8], (Q, D), 1.0, 6.0, ((0, 64), (1, 4)), jnp.float32)
    return dict(acts=acts, out_grad=out_grad, sample_rows=sample_rows, own_a=own_a, own_g=own_g, a_state=a_state, g_state=g_state, momentum=momentum, weight=weight)


factor_decay = 0.8
damping_rate = 0.03
momentum_rate = 0.9
decay_rate = 0.01
learn_rate = 0.05
epsilon_sq = 1e-06
highest = lax.Precision.HIGHEST

def newton_inverse(factor):
    width = factor.shape[-1]
    identity = jnp.eye(width, dtype=jnp.float32)
    trace_mean = jnp.trace(factor, axis1=-2, axis2=-1) / width
    damped = factor + damping_rate * trace_mean[:, None, None] * identity
    bound = lax.optimization_barrier(jnp.max(lax.optimization_barrier(jnp.sum(jnp.abs(damped), axis=-1)), axis=-1))
    guess = identity[None] / bound[:, None, None]
    for iteration in range(NS_IT):
        product = jnp.einsum('bij,bjk->bik', damped, guess, precision=highest)
        guess = jnp.einsum('bij,bjk->bik', guess, 2.0 * identity - product, precision=highest)
    return guess

def block_stats(rows, width):
    blocks = rows.astype(jnp.float32).reshape(rows.shape[0], -1, width)
    return jnp.einsum('sbi,sbj->bij', blocks, blocks)

def reference(acts, out_grad, sample_rows, own_a, own_g, a_state, g_state, momentum, weight):
    offsets = jnp.arange(SAMPLES, dtype=jnp.int32) // S_DEV * TOK_DEV
    picks = (offsets + sample_rows).astype(jnp.int32)
    stats_a = block_stats(acts[picks], BA).reshape(N_TENSOR, ABLK_T, BA, BA)
    stats_g = block_stats(out_grad[picks], BG).reshape(N_TENSOR, GBLK_T, BG, BG)
    groups = jnp.arange(N_TENSOR, dtype=jnp.int32)[:, None]
    fac_a = factor_decay * a_state[groups, own_a] + (1.0 - factor_decay) / SAMPLES * stats_a
    fac_g = factor_decay * g_state[groups, own_g] + (1.0 - factor_decay) / SAMPLES * stats_g
    a_new = jnp.zeros_like(a_state).at[groups, own_a].set(fac_a)
    g_new = jnp.zeros_like(g_state).at[groups, own_g].set(fac_g)
    inv_a = newton_inverse(fac_a.reshape(-1, BA, BA))
    inv_g = newton_inverse(fac_g.reshape(-1, BG, BG))
    raw_product = jnp.dot(out_grad.T, acts, preferred_element_type=jnp.float32)
    left_done = jnp.einsum('bij,bjd->bid', inv_g, raw_product.reshape(Q // BG, BG, D), precision=highest).reshape(Q, D)
    precon = jnp.einsum('qbi,bij->qbj', left_done.reshape(Q, D // BA, BA), inv_a, precision=highest).reshape(Q, D)
    mean_sq = jnp.mean(precon * precon)
    update = precon / jnp.sqrt(mean_sq + epsilon_sq)
    momentum_new = momentum_rate * momentum + update + decay_rate * weight
    weight_new = weight - learn_rate * momentum_new
    return (a_new, g_new, momentum_new, weight_new, weight_new.astype(jnp.bfloat16))
```

```python
import functools

import jax
import jax.numpy as jnp
from jax import lax
from jax.experimental import pallas as pl
from jax.experimental.pallas import tpu as pltpu
from jax.sharding import PartitionSpec as P

NS_IT = 5
NX = 4
NT = 4
BLK = 128

factor_decay = 0.8
damping_rate = 0.03
momentum_rate = 0.9
decay_rate = 0.01
learn_rate = 0.05
epsilon_sq = 1e-06

MESH = pl.DeviceIdType.MESH
f32 = jnp.float32
bf16 = jnp.bfloat16


def split(a):
    hi = a.astype(bf16)
    return hi, (a - hi.astype(f32)).astype(bf16)


def dot(a, b):
    return lax.dot_general(a, b, (((1,), (0,)), ((), ())), preferred_element_type=f32)


def dot3(a, b):
    ah, al = split(a)
    bh, bl = split(b)
    return dot(ah, bh) + (dot(ah, bl) + dot(al, bh))


def newton_inverses(factors, widths):
    rows = lax.broadcasted_iota(jnp.int32, (BLK, BLK), 0)
    cols = lax.broadcasted_iota(jnp.int32, (BLK, BLK), 1)
    identity = (rows == cols).astype(f32)
    damped, guess = [], []
    for factor, width in zip(factors, widths):
        inside = ((rows == cols) & (rows < width)).astype(f32)
        trace_mean = jnp.sum(jnp.sum(factor * inside, axis=1, keepdims=True), axis=0, keepdims=True) / width
        m = factor + (damping_rate * trace_mean) * inside
        bound = jnp.max(jnp.sum(jnp.abs(m), axis=1, keepdims=True), axis=0, keepdims=True)
        damped.append(split(m))
        guess.append(inside / bound)
    for _ in range(NS_IT):
        halves = [split(x) for x in guess]
        product = [
            dot(mh, xh) + (dot(mh, xl) + dot(ml, xh)) for (mh, ml), (xh, xl) in zip(damped, halves)
        ]
        rest = [split(2.0 * identity - p) for p in product]
        guess = [
            dot(xh, rh) + (dot(xh, rl) + dot(xl, rh)) for (xh, xl), (rh, rl) in zip(halves, rest)
        ]
    return guess


def kernel(
    nq, samples, entries,
    own_a, own_g, inv_own_a, inv_own_g,
    picks_a, picks_g, raw, a_state, g_state, momentum, weight,
    a_new, g_new, mom_new, w_new, gathered,
    pa_in, pg_in, raw_in, gst_in, part, parta_in, partg_in, red, fac, inv_g, fac_a, fac_g,
    st, st_in, both, out_buf, out_in, sq, sq_in, sq2, sq2_in, wide,
    s_pa, r_pa, s_pg, r_pg, s_raw, r_raw, s_gst, r_gst, s_rsa, r_rsa, s_rsg, r_rsg,
    s_aga, r_aga, s_agg, r_agg, s_faca, r_faca, s_invg, r_invg, s_facg, r_facg,
    s_st, r_st, s_out, r_out, s_sq, r_sq, s_sq2, r_sq2, s_w1, r_w1, s_w2, r_w2,
):
    h = lax.axis_index("shard")
    t = lax.axis_index("tensor")
    q = h // NX
    x = lax.rem(h, NX)
    s = h // nq
    j = lax.rem(h, nq)
    bg = g_state.shape[-1]
    group = 5 * bg

    def send(src, dst, ssem, rsem, shard, tensor):
        pltpu.make_async_remote_copy(
            src_ref=src, dst_ref=dst, send_sem=ssem, recv_sem=rsem,
            device_id={"shard": shard, "tensor": tensor}, device_id_type=MESH,
        ).start()

    def wait(ref, sem):
        pltpu.make_async_copy(ref, ref, sem).wait()

    def each(me, fn):
        def body(k, c):
            fn(lax.rem(me + k, nq))
            return c
        lax.fori_loop(1, nq, body, 0)

    def each_q(fn):
        each(q, lambda q2: fn(q2, q2 * NX + x))

    def each_j(fn):
        each(j, lambda j2: fn(j2, s * nq + j2))

    def each_x(fn):
        for k in (1, 3, 2):
            x2 = lax.rem(x + k, NX)
            fn(x2, q * NX + x2)

    def each_s(fn):
        for k in (2, 1, 3):
            s2 = lax.rem(s + k, NT)
            fn(s2, s2 * nq + j)

    def each_t(fn):
        for k in range(1, NT):
            fn(lax.rem(t + k, NT))

    def plane(fn):
        def body(k, c):
            other = lax.rem(s * NT + t + k, NT * NT)
            fn(other // NT * nq + j, lax.rem(other, NT))
            return c
        lax.fori_loop(1, NT * NT, body, 0)

    barrier = pltpu.get_barrier_semaphore()

    def greet(shard, tensor):
        pl.semaphore_signal(
            barrier, inc=1, device_id={"shard": shard, "tensor": tensor}, device_id_type=MESH
        )

    plane(greet)
    each_q(lambda q2, h2: greet(h2, t))
    each_j(lambda j2, h2: greet(h2, t))
    pl.semaphore_wait(barrier, NT * NT - 1 + 2 * (nq - 1))

    each_x(lambda x2, h2: send(picks_a.at[x2], pa_in.at[x], s_pa, r_pa, h2, t))
    each_s(lambda s2, h2: send(picks_g.at[s2], pg_in.at[s], s_pg, r_pg, h2, t))

    @pl.when(t == s)
    def _():
        each_t(lambda t2: send(g_state, gst_in, s_gst, r_gst, h, t2))

    def cols_of(x2):
        return raw.at[:, pl.ds(pl.multiple_of(x2 * BLK, BLK), BLK)]

    each_x(lambda x2, h2: send(cols_of(x2), raw_in.at[x], s_raw, r_raw, h2, t))

    @pl.when(t == s)
    def _():
        gst_in[...] = g_state[...]

    def square_sum(v):
        return lax.dot_general(v, v, (((0,), (0,)), ((), ())), preferred_element_type=f32)

    pa_in[pl.ds(x, 1)] = picks_a[pl.ds(x, 1)]
    pg_in[pl.ds(s, 1)] = picks_g[pl.ds(s, 1)]
    wait(pa_in.at[pl.ds(0, NX - 1)], r_pa)
    part[2 * BLK : 3 * BLK] = square_sum(pa_in[...].reshape(-1, BLK))
    pa = BLK // nq
    pg = 2 * BLK // nq

    def rows_a(ref, k):
        return ref.at[pl.ds(pl.multiple_of(2 * BLK + k * pa, 8), pa)]

    def rows_g(ref, k):
        return ref.at[pl.ds(pl.multiple_of(k * pg, 8), pg)]

    each_q(lambda q2, h2: send(rows_a(part, q2), parta_in.at[q], s_rsa, r_rsa, h2, t))
    wait(pg_in.at[pl.ds(0, NT - 1)], r_pg)
    for k in range(2):
        part[k * BLK : (k + 1) * BLK] = square_sum(
            pg_in[:, :, k * BLK : (k + 1) * BLK].reshape(-1, BLK)
        )
    each_j(lambda j2, h2: send(rows_g(part, j2), partg_in.at[j], s_rsg, r_rsg, h2, t))
    parta_in[pl.ds(q, 1)] = rows_a(part, q)[...][None]
    partg_in[pl.ds(j, 1)] = rows_g(part, j)[...][None]
    wait(parta_in.at[pl.ds(0, nq - 1)], r_rsa)
    rows_a(red, q)[...] = jnp.sum(parta_in[...], axis=0)
    each_q(lambda q2, h2: send(rows_a(red, q), rows_a(red, q), s_aga, r_aga, h2, t))
    wait(partg_in.at[pl.ds(0, nq - 1)], r_rsg)
    rows_g(red, j)[...] = jnp.sum(partg_in[...], axis=0)
    each_j(lambda j2, h2: send(rows_g(red, j), rows_g(red, j), s_agg, r_agg, h2, t))

    @pl.when(t != s)
    def _():
        wait(gst_in, r_gst)

    fresh_share = (1.0 - factor_decay) / samples
    fac[...] = jnp.zeros_like(fac)
    fac[0, 0:bg, 0:bg] = factor_decay * gst_in[own_g[s, t]]
    fac[1, 0:bg, 0:bg] = factor_decay * gst_in[own_g[s, 4]]
    fac[2] = factor_decay * a_state[own_a[t, x]]
    wait(parta_in.at[pl.ds(0, nq - 1)], r_aga)
    wait(partg_in.at[pl.ds(0, nq - 1)], r_agg)
    for k in range(3):
        fac[k] = fac[k] + fresh_share * red[k * BLK : (k + 1) * BLK, :]

    inverses = newton_inverses([fac[0], fac[1], fac[2]], [bg, bg, BLK])
    inv_g[pl.ds(t, 1)] = inverses[0][None]
    inv_g[4] = inverses[1]
    inv_a = inverses[2]
    each_t(lambda t2: send(inv_g.at[t], inv_g.at[t], s_invg, r_invg, h, t2))

    raw_in[pl.ds(x, 1)] = cols_of(x)[...][None]
    wait(raw_in.at[pl.ds(0, NX - 1)], r_raw)
    for k in range(NT):
        r = slice(k * group, (k + 1) * group)
        st[k] = (raw_in[0, r] + raw_in[1, r]) + (raw_in[2, r] + raw_in[3, r])
    each_s(lambda s2, h2: send(st.at[s2], st_in.at[s], s_st, r_st, h2, t))
    st_in[pl.ds(s, 1)] = st[pl.ds(s, 1)]

    each_x(lambda x2, h2: send(fac.at[2], fac_a.at[x], s_faca, r_faca, h2, t))
    fac_a[pl.ds(x, 1)] = fac[2][None]

    @pl.when(t == s)
    def _():
        each_s(lambda s2, h2: send(fac.at[0], fac_g.at[t], s_facg, r_facg, h2, s))
        each_s(lambda s2, h2: send(fac.at[1], fac_g.at[4], s_facg, r_facg, h2, s))
        fac_g[pl.ds(t, 1)] = fac[0][None]
        fac_g[4] = fac[1]

    @pl.when(t != s)
    def _():
        for s2 in range(NT):
            send(fac.at[0], fac_g.at[t], s_facg, r_facg, s2 * nq + j, s)

    wait(inv_g.at[pl.ds(0, NT - 1)], r_invg)
    wait(st_in.at[pl.ds(0, NT - 1)], r_st)
    ah, al = split(inv_a)
    for b in range(5):
        r = slice(b * bg, (b + 1) * bg)
        total = (st_in[0, r] + st_in[1, r]) + (st_in[2, r] + st_in[3, r])
        lh, ll = split(dot3(inv_g[b, 0:bg, 0:bg], total))
        both[r] = dot(lh, ah) + (dot(lh, al) + dot(ll, ah))
    own_rows = momentum.shape[0]
    wide_rows = out_buf.shape[1]
    for k in range(nq):
        out_buf[k, 0:own_rows] = both[k * own_rows : (k + 1) * own_rows]
        out_buf[k, own_rows:wide_rows] = jnp.zeros((wide_rows - own_rows, BLK), f32)
    each_j(lambda j2, h2: send(out_buf.at[j2], out_in.at[j], s_out, r_out, h2, t))
    out_in[pl.ds(j, 1)] = out_buf[pl.ds(j, 1)]
    wait(out_in.at[pl.ds(0, nq - 1)], r_out)
    square = jnp.zeros((8, BLK), f32)
    for b in range(NX):
        precon = jnp.zeros((wide_rows, BLK), f32)
        for k in range(b, nq, NX):
            precon = precon + out_in[k]
        wide[:, b * BLK : (b + 1) * BLK] = precon
        square = square + jnp.sum((precon * precon).reshape(-1, 8, BLK), axis=0)
    sq[...] = square
    each_j(lambda j2, h2: send(sq, sq_in.at[j], s_sq, r_sq, h2, t))
    sq_in[pl.ds(j, 1)] = square[None]
    wait(sq_in.at[pl.ds(0, nq - 1)], r_sq)
    sq2[...] = jnp.sum(sq_in[...], axis=0)
    plane(lambda h2, t2: send(sq2, sq2_in.at[s * NT + t], s_sq2, r_sq2, h2, t2))
    sq2_in[pl.ds(s * NT + t, 1)] = sq2[...][None]
    wait(sq2_in.at[pl.ds(0, NT * NT - 1)], r_sq2)
    total = jnp.sum(sq2_in[...], axis=0)
    mean_sq = jnp.sum(jnp.sum(total, axis=1, keepdims=True), axis=0, keepdims=True) / entries
    update = wide[0:own_rows] / jnp.sqrt(mean_sq + epsilon_sq)
    momentum_new = momentum_rate * momentum[...] + update + decay_rate * weight[...]
    weight_new = weight[...] - learn_rate * momentum_new
    mom_new[...] = momentum_new
    w_new[...] = weight_new
    wide[0:own_rows] = weight_new
    gathered[pl.ds(x, 1), pl.ds(q, 1)] = wide[...].astype(bf16)[None, None]
    mine = gathered.at[x, q]
    each_q(lambda q2, h2: send(mine, mine, s_w1, r_w1, h2, t))

    wait(fac_a.at[pl.ds(0, NX - 1)], r_faca)

    @pl.when(t == s)
    def _():
        wait(fac_g.at[pl.ds(0, 3)], r_facg)

    @pl.when(t != s)
    def _():
        wait(fac_g, r_facg)

    for k in range(4):
        a_new[k] = fac_a[inv_own_a[t, k]]
    for k in range(5):
        g_new[k] = fac_g[inv_own_g[t, k], 0:bg, 0:bg]

    wait(gathered.at[0, pl.ds(0, nq - 1)], r_w1)
    each_x(lambda x2, h2: send(gathered.at[x], gathered.at[x], s_w2, r_w2, h2, t))
    wait(gathered.at[pl.ds(0, NX - 1)], r_w2)

    wait(pa_in.at[pl.ds(0, NX - 1)], s_pa)
    wait(pg_in.at[pl.ds(0, NT - 1)], s_pg)
    wait(raw_in.at[pl.ds(0, NX - 1)], s_raw)

    @pl.when(t == s)
    def _():
        for _ in range(NT - 1):
            wait(gst_in, s_gst)
        for _ in range(2):
            wait(fac_g.at[pl.ds(0, 3)], s_facg)

    @pl.when(t != s)
    def _():
        wait(fac_g.at[pl.ds(0, 4)], s_facg)

    for sem in (s_rsa, s_aga):
        wait(parta_in.at[pl.ds(0, nq - 1)], sem)
    for sem in (s_rsg, s_agg):
        wait(partg_in.at[pl.ds(0, nq - 1)], sem)
    wait(inv_g.at[pl.ds(0, NT - 1)], s_invg)
    wait(fac_a.at[pl.ds(0, NX - 1)], s_faca)
    wait(st_in.at[pl.ds(0, NT - 1)], s_st)
    wait(out_in.at[pl.ds(0, nq - 1)], s_out)
    wait(sq_in.at[pl.ds(0, nq - 1)], s_sq)
    wait(sq2_in.at[pl.ds(0, NT * NT - 1)], s_sq2)
    wait(gathered.at[0, pl.ds(0, nq - 1)], s_w1)
    wait(gathered.at[pl.ds(0, NX - 1)], s_w2)


def local(acts, out_grad, sample_rows, own_a, own_g, a_state, g_state, momentum, weight):
    shard_count = lax.axis_size("shard")
    tensor_count = lax.axis_size("tensor")
    t = lax.axis_index("tensor")
    nq = shard_count // NX
    tokens, cols = acts.shape
    picked_rows = sample_rows.shape[0]
    out_dim = out_grad.shape[1]
    own_rows = momentum.shape[0]
    wide_rows = (own_rows + 15) // 16 * 16
    bg = g_state.shape[-1]

    pick = (sample_rows[:, None] == jnp.arange(tokens, dtype=jnp.int32)[None, :]).astype(bf16)
    picked_a = jnp.dot(pick, acts, preferred_element_type=f32).astype(bf16)
    picked_g = jnp.dot(pick, out_grad, preferred_element_type=f32).astype(bf16)
    picks_a = picked_a.reshape(picked_rows, NX, BLK).transpose(1, 0, 2)
    blocks_g = picked_g.reshape(picked_rows, NT, 5, bg).transpose(1, 0, 2, 3)
    g_mine = lax.dynamic_index_in_dim(blocks_g, t, 2, keepdims=False)
    pad = ((0, 0), (0, 0), (0, BLK - bg))
    picks_g = jnp.concatenate([jnp.pad(g_mine, pad), jnp.pad(blocks_g[:, :, 4], pad)], axis=-1)
    raw = lax.dot_general(
        out_grad, acts, (((0,), (0,)), ((), ())), preferred_element_type=f32
    )
    slots_a = jnp.arange(own_a.shape[1], dtype=jnp.int32)
    slots_g = jnp.arange(own_g.shape[1], dtype=jnp.int32)
    inv_own_a = jnp.sum(jnp.where(own_a[:, None, :] == slots_a[None, :, None], slots_a, 0), axis=-1)
    inv_own_g = jnp.sum(jnp.where(own_g[:, None, :] == slots_g[None, :, None], slots_g, 0), axis=-1)

    smem = pl.BlockSpec(memory_space=pltpu.SMEM)
    vmem = pl.BlockSpec(memory_space=pltpu.VMEM)
    group = out_dim // NX
    dma = pltpu.SemaphoreType.DMA
    a_new, g_new, mom_new, w_new, gathered = pl.pallas_call(
        functools.partial(
            kernel, nq, picked_rows * shard_count, own_rows * shard_count * cols * tensor_count
        ),
        out_shape=(
            jax.ShapeDtypeStruct(a_state.shape[1:], f32),
            jax.ShapeDtypeStruct(g_state.shape[1:], f32),
            jax.ShapeDtypeStruct(momentum.shape, f32),
            jax.ShapeDtypeStruct(weight.shape, f32),
            jax.ShapeDtypeStruct((NX, nq, wide_rows, cols), bf16),
        ),
        in_specs=[smem] * 4 + [vmem] * 7,
        out_specs=(vmem,) * 5,
        scratch_shapes=[
            pltpu.VMEM(picks_a.shape, bf16),
            pltpu.VMEM(picks_g.shape, bf16),
            pltpu.VMEM((NX, out_dim, BLK), f32),
            pltpu.VMEM(g_state.shape[1:], f32),
            pltpu.VMEM((3 * BLK, BLK), f32),
            pltpu.VMEM((nq, BLK // nq, BLK), f32),
            pltpu.VMEM((nq, 2 * BLK // nq, BLK), f32),
            pltpu.VMEM((3 * BLK, BLK), f32),
            pltpu.VMEM((3, BLK, BLK), f32),
            pltpu.VMEM((5, BLK, BLK), f32),
            pltpu.VMEM((NX, BLK, BLK), f32),
            pltpu.VMEM((5, BLK, BLK), f32),
            pltpu.VMEM((NT, group, BLK), f32),
            pltpu.VMEM((NT, group, BLK), f32),
            pltpu.VMEM((group, BLK), f32),
            pltpu.VMEM((nq, wide_rows, BLK), f32),
            pltpu.VMEM((nq, wide_rows, BLK), f32),
            pltpu.VMEM((8, BLK), f32),
            pltpu.VMEM((nq, 8, BLK), f32),
            pltpu.VMEM((8, BLK), f32),
            pltpu.VMEM((NT * NT, 8, BLK), f32),
            pltpu.VMEM((wide_rows, cols), f32),
        ]
        + [dma] * 34,
        compiler_params=pltpu.CompilerParams(
            collective_id=0, has_side_effects=True, vmem_limit_bytes=48 * 1024 * 1024
        ),
    )(own_a, own_g, inv_own_a, inv_own_g, picks_a, picks_g, raw, a_state[0], g_state[0], momentum, weight)
    full = gathered[:, :, :own_rows].transpose(1, 0, 2, 3).reshape(out_dim, cols)
    return (a_new[None], g_new[None], mom_new, w_new, full)


def solution(mesh):
    return jax.shard_map(
        local,
        mesh=mesh,
        in_specs=(
            P("shard", "tensor"),
            P("shard", None),
            P("shard"),
            P(),
            P(),
            P("tensor", None, None, None),
            P("tensor", None, None, None),
            P("shard", "tensor"),
            P("shard", "tensor"),
        ),
        out_specs=(
            P("tensor", None, None, None),
            P("tensor", None, None, None),
            P("shard", "tensor"),
            P("shard", "tensor"),
            P(None, "tensor"),
        ),
        check_vma=False,
    )
```

```python
import functools

import jax
import jax.numpy as jnp
from jax import lax
from jax.experimental import pallas as pl
from jax.experimental.pallas import tpu as pltpu
from jax.sharding import PartitionSpec as P

NS_IT = 5
NX = 4
NT = 4
BLK = 128

factor_decay = 0.8
damping_rate = 0.03
momentum_rate = 0.9
decay_rate = 0.01
learn_rate = 0.05
epsilon_sq = 1e-06

MESH = pl.DeviceIdType.MESH
f32 = jnp.float32
bf16 = jnp.bfloat16


def split(a):
    hi = a.astype(bf16)
    return hi, (a - hi.astype(f32)).astype(bf16)


def dot(a, b):
    return lax.dot_general(a, b, (((1,), (0,)), ((), ())), preferred_element_type=f32)


def dot3(a, b):
    ah, al = split(a)
    bh, bl = split(b)
    return dot(ah, bh) + (dot(ah, bl) + dot(al, bh))


def newton_inverses(factors, widths):
    rows = lax.broadcasted_iota(jnp.int32, (BLK, BLK), 0)
    cols = lax.broadcasted_iota(jnp.int32, (BLK, BLK), 1)
    identity = (rows == cols).astype(f32)
    damped, guess = [], []
    for factor, width in zip(factors, widths):
        inside = ((rows == cols) & (rows < width)).astype(f32)
        trace_mean = jnp.sum(jnp.sum(factor * inside, axis=1, keepdims=True), axis=0, keepdims=True) / width
        m = factor + (damping_rate * trace_mean) * inside
        bound = jnp.max(jnp.sum(jnp.abs(m), axis=1, keepdims=True), axis=0, keepdims=True)
        damped.append(split(m))
        guess.append(inside / bound)
    for _ in range(NS_IT):
        halves = [split(x) for x in guess]
        product = [
            dot(mh, xh) + (dot(mh, xl) + dot(ml, xh)) for (mh, ml), (xh, xl) in zip(damped, halves)
        ]
        rest = [split(2.0 * identity - p) for p in product]
        guess = [
            dot(xh, rh) + (dot(xh, rl) + dot(xl, rh)) for (xh, xl), (rh, rl) in zip(halves, rest)
        ]
    return guess


def kernel(
    nq, samples, entries,
    own_a, own_g, inv_own_a, inv_own_g,
    picks_a, picks_g, raw, a_state, g_state, momentum, weight,
    a_new, g_new, mom_new, w_new, gathered,
    pa_in, pg_in, raw_in, gst_in, part, parta_in, partg_in, red, fac, inv_g, fac_a, fac_g,
    st, st_in, both, out_buf, out_in, sq, sq_in, sq2, sq2_in, wide,
    s_pa, r_pa, s_pg, r_pg, s_raw, r_raw, s_gst, r_gst, s_rsa, r_rsa, s_rsg, r_rsg,
    s_aga, r_aga, s_agg, r_agg, s_faca, r_faca, s_invg, r_invg, s_facg, r_facg,
    s_st, r_st, s_out, r_out, s_sq, r_sq, s_sq2, r_sq2, s_w1, r_w1, s_w2, r_w2,
    r_relay, r_half,
):
    h = lax.axis_index("shard")
    t = lax.axis_index("tensor")
    q = h // NX
    x = lax.rem(h, NX)
    s = h // nq
    j = lax.rem(h, nq)
    bg = g_state.shape[-1]
    group = 5 * bg

    def send(src, dst, ssem, rsem, shard, tensor):
        pltpu.make_async_remote_copy(
            src_ref=src, dst_ref=dst, send_sem=ssem, recv_sem=rsem,
            device_id={"shard": shard, "tensor": tensor}, device_id_type=MESH,
        ).start()

    def wait(ref, sem):
        pltpu.make_async_copy(ref, ref, sem).wait()

    def each(me, fn):
        def body(k, c):
            fn(lax.rem(me + k, nq))
            return c
        lax.fori_loop(1, nq, body, 0)

    def each_q(fn):
        each(q, lambda q2: fn(q2, q2 * NX + x))

    def each_j(fn):
        each(j, lambda j2: fn(j2, s * nq + j2))

    def each_x(fn):
        for k in (1, 3, 2):
            x2 = lax.rem(x + k, NX)
            fn(x2, q * NX + x2)

    def each_s(fn):
        for k in (2, 1, 3):
            s2 = lax.rem(s + k, NT)
            fn(s2, s2 * nq + j)

    def each_t(fn):
        for k in range(1, NT):
            fn(lax.rem(t + k, NT))

    def plane(fn):
        def body(k, c):
            other = lax.rem(s * NT + t + k, NT * NT)
            fn(other // NT * nq + j, lax.rem(other, NT))
            return c
        lax.fori_loop(1, NT * NT, body, 0)

    barrier = pltpu.get_barrier_semaphore()

    def greet(shard, tensor):
        pl.semaphore_signal(
            barrier, inc=1, device_id={"shard": shard, "tensor": tensor}, device_id_type=MESH
        )

    plane(greet)
    each_q(lambda q2, h2: greet(h2, t))
    each_j(lambda j2, h2: greet(h2, t))
    pl.semaphore_wait(barrier, NT * NT - 1 + 2 * (nq - 1))

    each_x(lambda x2, h2: send(picks_a.at[x2], pa_in.at[x], s_pa, r_pa, h2, t))
    each_s(lambda s2, h2: send(picks_g.at[s2], pg_in.at[s], s_pg, r_pg, h2, t))

    @pl.when(t == s)
    def _():
        each_t(lambda t2: send(g_state, gst_in, s_gst, r_gst, h, t2))

    def cols_of(x2):
        return raw.at[:, pl.ds(pl.multiple_of(x2 * BLK, BLK), BLK)]

    right, left, across = (lax.rem(x + k, NX) for k in (1, 3, 2))
    h_right, h_left = q * NX + right, q * NX + left
    half = raw.shape[0] // 2
    top, bottom = pl.ds(0, half), pl.ds(half, half)

    def half_of(rows, x2):
        return raw.at[rows, pl.ds(pl.multiple_of(x2 * BLK, BLK), BLK)]

    send(half_of(top, across), raw_in.at[2, top], s_raw, r_relay, h_right, t)
    send(half_of(bottom, across), raw_in.at[2, bottom], s_raw, r_relay, h_left, t)

    @pl.when(t == s)
    def _():
        gst_in[...] = g_state[...]

    def square_sum(v):
        return lax.dot_general(v, v, (((0,), (0,)), ((), ())), preferred_element_type=f32)

    pa_in[pl.ds(x, 1)] = picks_a[pl.ds(x, 1)]
    pg_in[pl.ds(s, 1)] = picks_g[pl.ds(s, 1)]
    wait(pa_in.at[pl.ds(0, NX - 1)], r_pa)
    part[2 * BLK : 3 * BLK] = square_sum(pa_in[...].reshape(-1, BLK))
    pa = BLK // nq
    pg = 2 * BLK // nq

    def rows_a(ref, k):
        return ref.at[pl.ds(pl.multiple_of(2 * BLK + k * pa, 8), pa)]

    def rows_g(ref, k):
        return ref.at[pl.ds(pl.multiple_of(k * pg, 8), pg)]

    each_q(lambda q2, h2: send(rows_a(part, q2), parta_in.at[q], s_rsa, r_rsa, h2, t))
    wait(pg_in.at[pl.ds(0, NT - 1)], r_pg)
    for k in range(2):
        part[k * BLK : (k + 1) * BLK] = square_sum(
            pg_in[:, :, k * BLK : (k + 1) * BLK].reshape(-1, BLK)
        )
    each_j(lambda j2, h2: send(rows_g(part, j2), partg_in.at[j], s_rsg, r_rsg, h2, t))
    send(half_of(bottom, right), raw_in.at[0, bottom], s_raw, r_raw, h_right, t)
    send(half_of(top, left), raw_in.at[1, top], s_raw, r_raw, h_left, t)
    parta_in[pl.ds(q, 1)] = rows_a(part, q)[...][None]
    partg_in[pl.ds(j, 1)] = rows_g(part, j)[...][None]
    wait(parta_in.at[pl.ds(0, nq - 1)], r_rsa)
    rows_a(red, q)[...] = jnp.sum(parta_in[...], axis=0)
    each_q(lambda q2, h2: send(rows_a(red, q), rows_a(red, q), s_aga, r_aga, h2, t))
    wait(partg_in.at[pl.ds(0, nq - 1)], r_rsg)
    rows_g(red, j)[...] = jnp.sum(partg_in[...], axis=0)
    each_j(lambda j2, h2: send(rows_g(red, j), rows_g(red, j), s_agg, r_agg, h2, t))

    wait(raw_in.at[2], r_relay)
    raw_in[3, top] = raw_in[2, top] + half_of(top, right)[...]
    raw_in[3, bottom] = raw_in[2, bottom] + half_of(bottom, left)[...]
    send(raw_in.at[3, top], raw_in.at[0, top], s_raw, r_raw, h_right, t)
    send(raw_in.at[3, bottom], raw_in.at[1, bottom], s_raw, r_raw, h_left, t)

    @pl.when(t != s)
    def _():
        wait(gst_in, r_gst)

    fresh_share = (1.0 - factor_decay) / samples
    fac[...] = jnp.zeros_like(fac)
    fac[0, 0:bg, 0:bg] = factor_decay * gst_in[own_g[s, t]]
    fac[1, 0:bg, 0:bg] = factor_decay * gst_in[own_g[s, 4]]
    fac[2] = factor_decay * a_state[own_a[t, x]]
    wait(parta_in.at[pl.ds(0, nq - 1)], r_aga)
    wait(partg_in.at[pl.ds(0, nq - 1)], r_agg)
    for k in range(3):
        fac[k] = fac[k] + fresh_share * red[k * BLK : (k + 1) * BLK, :]

    inverses = newton_inverses([fac[0], fac[1], fac[2]], [bg, bg, BLK])
    inv_g[pl.ds(t, 1)] = inverses[0][None]
    inv_g[4] = inverses[1]
    inv_a = inverses[2]
    each_t(lambda t2: send(inv_g.at[t], inv_g.at[t], s_invg, r_invg, h, t2))

    wait(raw_in.at[pl.ds(0, 2)], r_raw)
    mine_raw = cols_of(x)
    for k in range(NT):
        r = slice(k * group, (k + 1) * group)
        st[k] = (raw_in[0, r] + raw_in[1, r]) + mine_raw[r]
    each_s(lambda s2, h2: send(st.at[s2], st_in.at[s], s_st, r_st, h2, t))
    st_in[pl.ds(s, 1)] = st[pl.ds(s, 1)]

    each_x(lambda x2, h2: send(fac.at[2], fac_a.at[x], s_faca, r_faca, h2, t))
    fac_a[pl.ds(x, 1)] = fac[2][None]

    @pl.when(t == s)
    def _():
        each_s(lambda s2, h2: send(fac.at[0], fac_g.at[t], s_facg, r_facg, h2, s))
        each_s(lambda s2, h2: send(fac.at[1], fac_g.at[4], s_facg, r_facg, h2, s))
        fac_g[pl.ds(t, 1)] = fac[0][None]
        fac_g[4] = fac[1]

    @pl.when(t != s)
    def _():
        for s2 in range(NT):
            send(fac.at[0], fac_g.at[t], s_facg, r_facg, s2 * nq + j, s)

    wait(inv_g.at[pl.ds(0, NT - 1)], r_invg)
    wait(st_in.at[pl.ds(0, NT - 1)], r_st)
    ah, al = split(inv_a)
    for b in range(5):
        r = slice(b * bg, (b + 1) * bg)
        total = (st_in[0, r] + st_in[1, r]) + (st_in[2, r] + st_in[3, r])
        lh, ll = split(dot3(inv_g[b, 0:bg, 0:bg], total))
        both[r] = dot(lh, ah) + (dot(lh, al) + dot(ll, ah))
    own_rows = momentum.shape[0]
    wide_rows = out_buf.shape[1]
    for k in range(nq):
        out_buf[k, 0:own_rows] = both[k * own_rows : (k + 1) * own_rows]
        out_buf[k, own_rows:wide_rows] = jnp.zeros((wide_rows - own_rows, BLK), f32)
    each_j(lambda j2, h2: send(out_buf.at[j2], out_in.at[j], s_out, r_out, h2, t))
    out_in[pl.ds(j, 1)] = out_buf[pl.ds(j, 1)]
    wait(out_in.at[pl.ds(0, nq - 1)], r_out)
    square = jnp.zeros((8, BLK), f32)
    for b in range(NX):
        precon = jnp.zeros((wide_rows, BLK), f32)
        for k in range(b, nq, NX):
            precon = precon + out_in[k]
        wide[:, b * BLK : (b + 1) * BLK] = precon
        square = square + jnp.sum((precon * precon).reshape(-1, 8, BLK), axis=0)
    sq[...] = square
    each_j(lambda j2, h2: send(sq, sq_in.at[j], s_sq, r_sq, h2, t))
    sq_in[pl.ds(j, 1)] = square[None]
    wait(sq_in.at[pl.ds(0, nq - 1)], r_sq)
    sq2[...] = jnp.sum(sq_in[...], axis=0)
    plane(lambda h2, t2: send(sq2, sq2_in.at[s * NT + t], s_sq2, r_sq2, h2, t2))
    sq2_in[pl.ds(s * NT + t, 1)] = sq2[...][None]
    wait(sq2_in.at[pl.ds(0, NT * NT - 1)], r_sq2)
    total = jnp.sum(sq2_in[...], axis=0)
    mean_sq = jnp.sum(jnp.sum(total, axis=1, keepdims=True), axis=0, keepdims=True) / entries
    update = wide[0:own_rows] / jnp.sqrt(mean_sq + epsilon_sq)
    momentum_new = momentum_rate * momentum[...] + update + decay_rate * weight[...]
    weight_new = weight[...] - learn_rate * momentum_new
    mom_new[...] = momentum_new
    w_new[...] = weight_new
    wide[0:own_rows] = weight_new
    gathered[pl.ds(x, 1), pl.ds(q, 1)] = wide[...].astype(bf16)[None, None]
    mine = gathered.at[x, q]
    each_q(lambda q2, h2: send(mine, mine, s_w1, r_w1, h2, t))

    wait(fac_a.at[pl.ds(0, NX - 1)], r_faca)

    @pl.when(t == s)
    def _():
        wait(fac_g.at[pl.ds(0, 3)], r_facg)

    @pl.when(t != s)
    def _():
        wait(fac_g, r_facg)

    for k in range(4):
        a_new[k] = fac_a[inv_own_a[t, k]]
    for k in range(5):
        g_new[k] = fac_g[inv_own_g[t, k], 0:bg, 0:bg]

    wait(gathered.at[0, pl.ds(0, nq - 1)], r_w1)
    first, second = pl.ds(0, nq // 2), pl.ds(nq // 2, nq // 2)

    def spread(x2, part_q, rsem, shard):
        send(gathered.at[x2, part_q], gathered.at[x2, part_q], s_w2, rsem, shard, t)

    spread(x, first, r_half, h_right)
    spread(x, second, r_half, h_left)
    spread(x, second, r_w2, h_right)
    spread(x, first, r_w2, h_left)
    wait(gathered.at[0], r_half)
    spread(left, first, r_w2, h_right)
    spread(right, second, r_w2, h_left)
    wait(gathered.at[pl.ds(0, 2)], r_w2)

    wait(pa_in.at[pl.ds(0, NX - 1)], s_pa)
    wait(pg_in.at[pl.ds(0, NT - 1)], s_pg)
    wait(raw_in.at[pl.ds(0, NX - 1)], s_raw)

    @pl.when(t == s)
    def _():
        for _ in range(NT - 1):
            wait(gst_in, s_gst)
        for _ in range(2):
            wait(fac_g.at[pl.ds(0, 3)], s_facg)

    @pl.when(t != s)
    def _():
        wait(fac_g.at[pl.ds(0, 4)], s_facg)

    for sem in (s_rsa, s_aga):
        wait(parta_in.at[pl.ds(0, nq - 1)], sem)
    for sem in (s_rsg, s_agg):
        wait(partg_in.at[pl.ds(0, nq - 1)], sem)
    wait(inv_g.at[pl.ds(0, NT - 1)], s_invg)
    wait(fac_a.at[pl.ds(0, NX - 1)], s_faca)
    wait(st_in.at[pl.ds(0, NT - 1)], s_st)
    wait(out_in.at[pl.ds(0, nq - 1)], s_out)
    wait(sq_in.at[pl.ds(0, nq - 1)], s_sq)
    wait(sq2_in.at[pl.ds(0, NT * NT - 1)], s_sq2)
    wait(gathered.at[0, pl.ds(0, nq - 1)], s_w1)
    wait(gathered.at[pl.ds(0, NX - 1)], s_w2)


def local(acts, out_grad, sample_rows, own_a, own_g, a_state, g_state, momentum, weight):
    shard_count = lax.axis_size("shard")
    tensor_count = lax.axis_size("tensor")
    t = lax.axis_index("tensor")
    nq = shard_count // NX
    tokens, cols = acts.shape
    picked_rows = sample_rows.shape[0]
    out_dim = out_grad.shape[1]
    own_rows = momentum.shape[0]
    wide_rows = (own_rows + 15) // 16 * 16
    bg = g_state.shape[-1]

    pick = (sample_rows[:, None] == jnp.arange(tokens, dtype=jnp.int32)[None, :]).astype(bf16)
    picked_a = jnp.dot(pick, acts, preferred_element_type=f32).astype(bf16)
    picked_g = jnp.dot(pick, out_grad, preferred_element_type=f32).astype(bf16)
    picks_a = picked_a.reshape(picked_rows, NX, BLK).transpose(1, 0, 2)
    blocks_g = picked_g.reshape(picked_rows, NT, 5, bg).transpose(1, 0, 2, 3)
    g_mine = lax.dynamic_index_in_dim(blocks_g, t, 2, keepdims=False)
    pad = ((0, 0), (0, 0), (0, BLK - bg))
    picks_g = jnp.concatenate([jnp.pad(g_mine, pad), jnp.pad(blocks_g[:, :, 4], pad)], axis=-1)
    raw = lax.dot_general(
        out_grad, acts, (((0,), (0,)), ((), ())), preferred_element_type=f32
    )
    slots_a = jnp.arange(own_a.shape[1], dtype=jnp.int32)
    slots_g = jnp.arange(own_g.shape[1], dtype=jnp.int32)
    inv_own_a = jnp.sum(jnp.where(own_a[:, None, :] == slots_a[None, :, None], slots_a, 0), axis=-1)
    inv_own_g = jnp.sum(jnp.where(own_g[:, None, :] == slots_g[None, :, None], slots_g, 0), axis=-1)

    smem = pl.BlockSpec(memory_space=pltpu.SMEM)
    vmem = pl.BlockSpec(memory_space=pltpu.VMEM)
    group = out_dim // NX
    dma = pltpu.SemaphoreType.DMA
    a_new, g_new, mom_new, w_new, gathered = pl.pallas_call(
        functools.partial(
            kernel, nq, picked_rows * shard_count, own_rows * shard_count * cols * tensor_count
        ),
        out_shape=(
            jax.ShapeDtypeStruct(a_state.shape[1:], f32),
            jax.ShapeDtypeStruct(g_state.shape[1:], f32),
            jax.ShapeDtypeStruct(momentum.shape, f32),
            jax.ShapeDtypeStruct(weight.shape, f32),
            jax.ShapeDtypeStruct((NX, nq, wide_rows, cols), bf16),
        ),
        in_specs=[smem] * 4 + [vmem] * 7,
        out_specs=(vmem,) * 5,
        scratch_shapes=[
            pltpu.VMEM(picks_a.shape, bf16),
            pltpu.VMEM(picks_g.shape, bf16),
            pltpu.VMEM((NX, out_dim, BLK), f32),
            pltpu.VMEM(g_state.shape[1:], f32),
            pltpu.VMEM((3 * BLK, BLK), f32),
            pltpu.VMEM((nq, BLK // nq, BLK), f32),
            pltpu.VMEM((nq, 2 * BLK // nq, BLK), f32),
            pltpu.VMEM((3 * BLK, BLK), f32),
            pltpu.VMEM((3, BLK, BLK), f32),
            pltpu.VMEM((5, BLK, BLK), f32),
            pltpu.VMEM((NX, BLK, BLK), f32),
            pltpu.VMEM((5, BLK, BLK), f32),
            pltpu.VMEM((NT, group, BLK), f32),
            pltpu.VMEM((NT, group, BLK), f32),
            pltpu.VMEM((group, BLK), f32),
            pltpu.VMEM((nq, wide_rows, BLK), f32),
            pltpu.VMEM((nq, wide_rows, BLK), f32),
            pltpu.VMEM((8, BLK), f32),
            pltpu.VMEM((nq, 8, BLK), f32),
            pltpu.VMEM((8, BLK), f32),
            pltpu.VMEM((NT * NT, 8, BLK), f32),
            pltpu.VMEM((wide_rows, cols), f32),
        ]
        + [dma] * 36,
        compiler_params=pltpu.CompilerParams(
            collective_id=0, has_side_effects=True, vmem_limit_bytes=48 * 1024 * 1024
        ),
    )(own_a, own_g, inv_own_a, inv_own_g, picks_a, picks_g, raw, a_state[0], g_state[0], momentum, weight)
    full = gathered[:, :, :own_rows].transpose(1, 0, 2, 3).reshape(out_dim, cols)
    return (a_new[None], g_new[None], mom_new, w_new, full)


def solution(mesh):
    return jax.shard_map(
        local,
        mesh=mesh,
        in_specs=(
            P("shard", "tensor"),
            P("shard", None),
            P("shard"),
            P(),
            P(),
            P("tensor", None, None, None),
            P("tensor", None, None, None),
            P("shard", "tensor"),
            P("shard", "tensor"),
        ),
        out_specs=(
            P("tensor", None, None, None),
            P("tensor", None, None, None),
            P("shard", "tensor"),
            P("shard", "tensor"),
            P(None, "tensor"),
        ),
        check_vma=False,
    )
```
